128 devices in a mesh: seq: 64 (over y, z, x_hi, core), head: 2 (over x_lo).
Axes of the slice: x: 4 (x_hi: 2, x_lo: 2; x = x_hi * 2 + x_lo), y: 4, z: 4, core: 2. Of those that a mesh axis runs over, the one named last changes fastest.
Arguments:
- queries: bfloat16 [2, 16384, 2048], P(None, 'seq', 'head'), may hold values from -8 to 8
- key_states: bfloat16 [2, 16384, 2048], P(None, 'seq', 'head'), may hold values from -8 to 8
- value_states: bfloat16 [2, 16384, 2048], P(None, 'seq', 'head'), may hold values from -6 to 6
- output_grad: bfloat16 [2, 16384, 2048], P(None, 'seq', 'head'), may hold values from -6 to 6
- out_proj: bfloat16 [2048, 2048], P('head'), may hold values from -0.125 to 0.125
Outputs:
- layer_out: bfloat16 [2, 16384, 2048], P(None, 'seq', 'head')
- query_grad: bfloat16 [2, 16384, 2048], P(None, 'seq', 'head')
- key_grad: bfloat16 [2, 16384, 2048], P(None, 'seq', 'head')
- value_grad: bfloat16 [2, 16384, 2048], P(None, 'seq', 'head')
The draws below stay inside these ranges and needn't reach their ends.
All inputs are finite; a program needn't handle non-finite values.
Results may differ from the reference program's by a relative error of at most 0.012.
The reference program's roundings to bfloat16 on the way count: a program that leaves them out, or rounds other values in their place, can miss the bound.
Values may be sent and summed in bfloat16 or wider, within the bound.
A program may use at most 192 MiB of HBM per device.

```python
import jax
import jax.numpy as jnp
from jax import lax

HEADS = 16
HEAD_DIM = 128
BLOCK = 256
BATCH = 2
SEQ = 16384
N_SEQ = 64


def base_draw(key, salt):
    full_shape = (BATCH, SEQ, HEADS * HEAD_DIM)
    return jnp.clip(jax.random.normal(jax.random.fold_in(key, salt), full_shape, jnp.float32), -4.0, 4.0)


def draw_queries(key, part):
    drawn = base_draw(key, 1)
    return drawn.astype(jnp.bfloat16)


def draw_key_states(key, part):
    drawn = base_draw(key, 2)
    return drawn.astype(jnp.bfloat16)


def steps_of(stream_key, dims, pieces, smallest, high):
    loudness, own = 1.0, jax.random.fold_in(stream_key, 6)
    for axis_at, shards_of in pieces:
        draws = jnp.exp(jax.random.uniform(jax.random.fold_in(own, axis_at), (shards_of,), jnp.float32, smallest / len(pieces), high / len(pieces)))
        loudness = loudness * jnp.repeat(draws, dims[axis_at] // shards_of).reshape([-1 if axis == axis_at else 1 for axis in range(len(dims))])
    return loudness


def scatter_about(own_key, shape, deviation, reach, shards=(), kind=jnp.bfloat16):
    gain = steps_of(own_key, shape, shards, -0.22, 0.18) if shards else 1.0
    drawn = jax.random.normal(own_key, shape, jnp.float32) * deviation * gain
    return jnp.minimum(jnp.maximum(drawn, -reach), reach).astype(kind)


def setup_inputs(seed: int = 0) -> dict:
    key_list = jax.random.split(jax.random.key(seed), 6)
    return {
        "queries": draw_queries(jax.random.fold_in(key_list[5], 71), 0),
        "key_states": draw_key_states(jax.random.fold_in(key_list[5], 71), 0),
        "value_states": scatter_about(key_list[2], (BATCH, SEQ, HEADS * HEAD_DIM), 1.0, 6.0, ((1, 64), (2, 2))),
        "output_grad": scatter_about(key_list[3], (BATCH, SEQ, HEADS * HEAD_DIM), 1.0, 6.0, ((1, 64), (2, 2))),
        "out_proj": scatter_about(key_list[4], (HEADS * HEAD_DIM, HEADS * HEAD_DIM), (HEADS * HEAD_DIM) ** -0.5, 0.125, ((0, 2),)),
    }


def rounded(value):
    return lax.optimization_barrier(value.astype(jnp.bfloat16)).astype(jnp.float32)


def reference(queries, key_states, value_states, output_grad, out_proj):
    score_scale = HEAD_DIM ** -0.5
    levels = N_SEQ.bit_length() - 1
    width = HEADS * HEAD_DIM
    batch = queries.shape[0]
    num_blocks = SEQ // BLOCK
    attn_flat = jnp.dot(output_grad.reshape(-1, width), out_proj.T, preferred_element_type=jnp.float32)
    attn_grad = attn_flat.astype(jnp.bfloat16).reshape(batch, SEQ, width)
    causal = jnp.arange(BLOCK)[:, None] >= jnp.arange(BLOCK)[None, :]

    def rows_of(source, block_index):
        start = (block_index * BLOCK).astype(jnp.int32)
        piece = lax.dynamic_slice_in_dim(source, start, BLOCK, 1)
        return piece.reshape(batch, BLOCK, HEADS, HEAD_DIM).astype(jnp.float32)

    def add_rows(total, block_index, term):
        start = (block_index * BLOCK).astype(jnp.int32)
        current = lax.dynamic_slice_in_dim(total, start, BLOCK, 1)
        return lax.dynamic_update_slice_in_dim(total, current + term, start, 1)

    def one_block(block_index, state_tuple):
        attention, query_grad, key_total, value_total = state_tuple
        block_index = jnp.asarray(block_index).astype(jnp.int32)
        partners = [jnp.bitwise_xor(block_index, 1 << depth_index).astype(jnp.int32) for depth_index in range(levels)]
        seen = [block_index] + partners
        key_row_block = jnp.concatenate([rows_of(key_states, item) for item in seen], axis=1)
        value_row_block = jnp.concatenate([rows_of(value_states, item) for item in seen], axis=1)
        query_row_block = rows_of(queries, block_index)
        gradient_row_block = rows_of(attn_grad, block_index)
        key_mask = jnp.concatenate([causal] + [jnp.broadcast_to(item < block_index, (BLOCK, BLOCK)) for item in partners], axis=1)
        scores = jnp.einsum('bqhd,bkhd->bhqk', query_row_block, key_row_block) * score_scale
        scores = jnp.where(key_mask, scores, -jnp.inf)
        maxima = jnp.max(scores, axis=3, keepdims=True)
        log_norm = maxima + jnp.log(jnp.sum(jnp.exp(scores - maxima), axis=3, keepdims=True))
        weights = jnp.exp(scores - log_norm)
        lower_weight_block = rounded(weights)
        attn_block = jnp.einsum('bhqk,bkhd->bqhd', lower_weight_block, value_row_block).astype(jnp.bfloat16)
        row_dsum = jnp.sum(gradient_row_block * attn_block.astype(jnp.float32), axis=3)
        grad_weights = jnp.einsum('bqhd,bkhd->bhqk', gradient_row_block, value_row_block)
        score_gradients = rounded(weights * (grad_weights - jnp.transpose(row_dsum, (0, 2, 1))[..., None]))
        dquery = (jnp.einsum('bhqk,bkhd->bqhd', score_gradients, key_row_block) * score_scale).astype(jnp.bfloat16)
        key_term = jnp.einsum('bhqk,bqhd->bkhd', score_gradients, query_row_block) * score_scale
        value_term = jnp.einsum('bhqk,bqhd->bkhd', lower_weight_block, gradient_row_block)
        start = (block_index * BLOCK).astype(jnp.int32)
        attention = lax.dynamic_update_slice_in_dim(attention, attn_block, start, 1)
        query_grad = lax.dynamic_update_slice_in_dim(query_grad, dquery, start, 1)
        key_total = add_rows(key_total, block_index, key_term[:, :BLOCK])
        value_total = add_rows(value_total, block_index, value_term[:, :BLOCK])
        for depth_index in range(levels):
            low = (depth_index + 1) * BLOCK
            key_total = add_rows(key_total, partners[depth_index], rounded(key_term[:, low:low + BLOCK]))
            value_total = add_rows(value_total, partners[depth_index], rounded(value_term[:, low:low + BLOCK]))
        return attention, query_grad, key_total, value_total

    head_shape = (batch, SEQ, HEADS, HEAD_DIM)
    start_state = (jnp.zeros(head_shape, jnp.bfloat16), jnp.zeros(head_shape, jnp.bfloat16), jnp.zeros(head_shape, jnp.float32), jnp.zeros(head_shape, jnp.float32))
    attention, query_grad, key_total, value_total = lax.fori_loop(0, num_blocks, one_block, start_state)
    layer_out = jnp.dot(attention.reshape(-1, width), out_proj, preferred_element_type=jnp.float32)
    layer_out = layer_out.astype(jnp.bfloat16).reshape(batch, SEQ, width)
    return (layer_out, query_grad.reshape(batch, SEQ, width), key_total.astype(jnp.bfloat16).reshape(batch, SEQ, width), value_total.astype(jnp.bfloat16).reshape(batch, SEQ, width))
```

```python
from functools import partial

import jax
import jax.numpy as jnp
from jax import lax
from jax.sharding import PartitionSpec as P

HEAD_DIM = 128


def passed_along(shard, axis, by):
    length = lax.axis_size(axis)
    pairs = [(i, i ^ abs(by)) for i in range(length) if ((i & abs(by)) == 0) == (by > 0)]
    return lax.ppermute(shard, axis, pairs)


def head_major(source):
    batch_rows, token_rows, features = source.shape
    return jnp.transpose(
        source.reshape(batch_rows, token_rows, features // HEAD_DIM, HEAD_DIM), (2, 0, 1, 3)
    )


def row_major(source):
    head_count, batch_rows, token_rows, features = source.shape
    return jnp.transpose(source, (1, 2, 0, 3)).reshape(
        batch_rows, token_rows, head_count * features
    )


def head_pass(pieces, key_mask, score_scale, whole):
    query_row_block, key_row_block, value_row_block, gradient_row_block = pieces
    own_rows = query_row_block.shape[1]
    scores = (
        jnp.einsum(
            "xei,xgi->xeg", query_row_block, key_row_block, preferred_element_type=jnp.float32
        )
        * score_scale
    )
    scores = jnp.where(key_mask, scores, -jnp.inf)
    maxima = jnp.max(scores, axis=2, keepdims=True)
    log_norm = maxima + jnp.log(jnp.sum(jnp.exp(scores - maxima), axis=2, keepdims=True))
    weights = jnp.exp(scores - log_norm)
    lower_weight_block = weights.astype(jnp.bfloat16)
    attn_block = jnp.einsum(
        "ifj,ijx->ifx", lower_weight_block, value_row_block, preferred_element_type=jnp.float32
    ).astype(jnp.bfloat16)
    row_dsum = jnp.sum(
        gradient_row_block.astype(jnp.float32) * attn_block.astype(jnp.float32),
        axis=2,
        keepdims=True,
    )
    grad_weights = jnp.einsum(
        "xei,xgi->xeg", gradient_row_block, value_row_block, preferred_element_type=jnp.float32
    )
    score_gradients = (weights * (grad_weights - row_dsum)).astype(jnp.bfloat16)
    dquery = (
        jnp.einsum(
            "ifj,ijx->ifx", score_gradients, key_row_block, preferred_element_type=jnp.float32
        )
        * score_scale
    ).astype(jnp.bfloat16)
    key_term = (
        jnp.einsum(
            "uwp,uwf->upf", score_gradients, query_row_block, preferred_element_type=jnp.float32
        )
        * score_scale
    )
    value_term = jnp.einsum(
        "uwp,uwf->upf", lower_weight_block, gradient_row_block, preferred_element_type=jnp.float32
    )
    return (
        attn_block,
        dquery,
        key_term[:, :own_rows],
        value_term[:, :own_rows],
        key_term[:, own_rows:].astype(jnp.bfloat16),
        value_term[:, own_rows:].astype(jnp.bfloat16),
    )


def body(queries, key_states, value_states, output_grad, out_proj):
    score_scale = HEAD_DIM ** (-0.5)
    levels = lax.axis_size("seq").bit_length() - 1
    seq_place = lax.axis_index("seq")
    own_rows = queries.shape[1]
    attn_grad = jnp.einsum(
        "brf,df->brd",
        lax.all_gather(output_grad, "head", axis=2, tiled=True),
        out_proj,
        preferred_element_type=jnp.float32,
    ).astype(jnp.bfloat16)
    causal = jnp.arange(own_rows)[:, None] >= jnp.arange(own_rows)[None, :]
    partner_flags = [seq_place // 2**bit_index % 2 == 1 for bit_index in range(levels)]
    key_mask = jnp.concatenate(
        [causal]
        + [jnp.broadcast_to(flag_value, (own_rows, own_rows)) for flag_value in partner_flags],
        axis=1,
    )
    key_parts = [key_states]
    value_parts = [value_states]
    for bit_index in range(levels):
        far_key, far_value = passed_along((key_states, value_states), "seq", 2**bit_index)
        key_parts.append(far_key)
        value_parts.append(far_value)
    pieces = (
        head_major(queries),
        head_major(jnp.concatenate(key_parts, axis=1)),
        head_major(jnp.concatenate(value_parts, axis=1)),
        head_major(attn_grad),
    )
    attn_heads, dquery_heads, own_key, own_value, far_keys, far_values = lax.map(
        partial(head_pass, key_mask=key_mask, score_scale=score_scale, whole=True), pieces
    )
    key_total = row_major(own_key)
    value_total = row_major(own_value)
    for bit_index in range(levels):
        low = bit_index * own_rows
        sent_key = row_major(far_keys[:, :, low : low + own_rows])
        sent_value = row_major(far_values[:, :, low : low + own_rows])
        back_key, back_value = passed_along((sent_key, sent_value), "seq", -(2**bit_index))
        key_total = key_total + back_key.astype(jnp.float32)
        value_total = value_total + back_value.astype(jnp.float32)
    attn_rows = row_major(attn_heads)
    query_grad = row_major(dquery_heads)
    partial_out = jnp.einsum("brd,df->brf", attn_rows, out_proj, preferred_element_type=jnp.float32)
    layer_out = lax.psum_scatter(partial_out, "head", scatter_dimension=2, tiled=True).astype(
        jnp.bfloat16
    )
    return (layer_out, query_grad, key_total.astype(jnp.bfloat16), value_total.astype(jnp.bfloat16))


def solution(mesh):
    in_specs = (
        P(None, "seq", "head"),
        P(None, "seq", "head"),
        P(None, "seq", "head"),
        P(None, "seq", "head"),
        P("head", None),
    )
    out_specs = (
        P(None, "seq", "head"),
        P(None, "seq", "head"),
        P(None, "seq", "head"),
        P(None, "seq", "head"),
    )
    return jax.shard_map(body, mesh=mesh, in_specs=in_specs, out_specs=out_specs, check_vma=False)
```

```python
import functools
import math

import jax
import jax.numpy as jnp
from jax import lax
from jax.experimental import pallas as pl
from jax.experimental.pallas import tpu as pltpu
from jax.sharding import PartitionSpec as P

HEAD_DIM = 128
GROUP = 2
MESH = pl.DeviceIdType.MESH
F32 = jnp.float32
BF16 = jnp.bfloat16
LOW = -1e30
TILE = 32


def dot_nt(a, b):
    return lax.dot_general(a, b, (((1,), (1,)), ((), ())), preferred_element_type=F32)


def dot_nn(a, b):
    return lax.dot_general(a, b, (((1,), (0,)), ((), ())), preferred_element_type=F32)


def dot_tn(a, b):
    return lax.dot_general(a, b, (((0,), (0,)), ((), ())), preferred_element_type=F32)


def kernel(
    levels, q_in, k_in, v_in, og_in, w_in, lo_out, dq_out, dk_out, dv_out,
    q, kv, far, do, w, og, og_far, attn, s, p, dp, ds, top, norm, acc, own, dq, po, po_far, lo,
    ld_q, ld_kv, ld_og, ld_w, og_send, og_recv, po_send, po_recv, kv_send, kv_recv, out_sem, grad_sem,
):
    me = lax.axis_index("seq")
    hd = lax.axis_index("head")
    chunks, rows, width = q.shape
    batch = og.shape[0]
    half = og.shape[2]
    per = chunks // batch
    scale = HEAD_DIM ** -0.5
    rate = scale * math.log2(math.e)
    own_cols = pl.multiple_of(hd * half, half)
    far_cols = pl.multiple_of((1 - hd) * half, half)

    def bit(j):
        return lax.rem(lax.shift_right_logical(me, j), 2)

    def partner(j):
        return me + (1 - 2 * bit(j)) * (1 << j)

    def cols(c):
        return pl.ds(pl.multiple_of(lax.rem(c, per) * width, width), width)

    def load_kv(c, i):
        src = (k_in, v_in)[i].at[lax.div(c, per), :, cols(c)]
        return pltpu.make_async_copy(src, kv.at[c, i], ld_kv.at[c, i])

    def load_q(c):
        return pltpu.make_async_copy(q_in.at[lax.div(c, per), :, cols(c)], q.at[c], ld_q.at[c])

    def load_og(b):
        return pltpu.make_async_copy(og_in.at[b], og.at[b], ld_og.at[b])

    load_w = pltpu.make_async_copy(w_in, w, ld_w)

    def send_og(b):
        return pltpu.make_async_remote_copy(
            og_in.at[b], og_far.at[b], og_send.at[b], og_recv.at[b],
            device_id=(me, 1 - hd), device_id_type=MESH)

    def send_po(b):
        return pltpu.make_async_remote_copy(
            po.at[b], po_far.at[b], po_send.at[b], po_recv.at[b],
            device_id=(me, 1 - hd), device_id_type=MESH)

    def send_kv(j, c):
        return pltpu.make_async_remote_copy(
            kv.at[c], far.at[j, c], kv_send.at[j, c], kv_recv.at[j, c],
            device_id=(partner(j), hd), device_id_type=MESH)

    def send_grad(j, c):
        return pltpu.make_async_remote_copy(
            far.at[j, c], far.at[j, c], kv_send.at[j, c], kv_recv.at[j, c],
            device_id=(partner(j), hd), device_id_type=MESH)

    def put_dq(c):
        return pltpu.make_async_copy(dq.at[c], dq_out.at[lax.div(c, per), :, cols(c)], out_sem.at[c])

    def put_grad(c, i):
        dst = (dk_out, dv_out)[i].at[lax.div(c, per), :, cols(c)]
        return pltpu.make_async_copy(kv.at[c, i], dst, grad_sem.at[c, i])

    def start_loads(c, carry):
        load_kv(c, 0).start()
        load_kv(c, 1).start()
        return carry

    lax.fori_loop(0, chunks, start_loads, 0)
    for b in range(batch):
        load_og(b).start()

    def start_q(c, carry):
        load_q(c).start()
        return carry

    lax.fori_loop(0, chunks, start_q, 0)
    load_w.start()

    barrier = pltpu.get_barrier_semaphore()
    for j in range(levels):
        pl.semaphore_signal(barrier, inc=1, device_id=(partner(j), hd), device_id_type=MESH)
    pl.semaphore_signal(barrier, inc=1, device_id=(me, 1 - hd), device_id_type=MESH)
    pl.semaphore_wait(barrier, levels + 1)

    send_og(0).start()

    def start_sends(c, carry):
        load_kv(c, 0).wait()
        load_kv(c, 1).wait()
        for j in range(levels):
            @pl.when(bit(j) == 0)
            def _():
                send_kv(j, c).start()

        if batch > 1:
            @pl.when(c == 1)
            def _():
                for b in range(1, batch):
                    send_og(b).start()
        return carry

    lax.fori_loop(0, chunks, start_sends, 0)
    for b in range(batch):
        load_og(b).wait()
    lax.fori_loop(0, chunks, lambda c, carry: (load_q(c).wait(), carry)[1], 0)
    load_w.wait()

    heads = [slice(u * HEAD_DIM, (u + 1) * HEAD_DIM) for u in range(GROUP)]
    tiles = [slice(t, t + TILE) for t in range(0, rows, TILE)]

    def absorb(slot, u):
        peak = s[slot, u, tiles[0], :]
        for t in tiles[1:]:
            peak = jnp.maximum(peak, s[slot, u, t, :])
        old = top[u]
        new = jnp.maximum(old, jnp.max(peak, axis=0, keepdims=True))
        total = None
        for t in tiles:
            e = jnp.exp2((s[slot, u, t, :] - new) * rate)
            total = e if total is None else total + e
        norm[u] = norm[u] * jnp.exp2((old - new) * rate) + jnp.sum(total, axis=0, keepdims=True)
        top[u] = new

    def weigh(slot, u, value_ref):
        shift = norm[u]
        for t in tiles:
            e = jnp.exp2(s[slot, u, t, :] * rate - shift)
            s[slot, u, t, :] = e
            p[slot, u, t, :] = e.astype(BF16)
        acc[u] += dot_tn(value_ref[:, heads[u]], p[slot, u])

    def back(slot, u, c, key_ref, value_ref):
        dsum = norm[u]
        dp[u] = dot_nt(value_ref[:, heads[u]], do[c, :, heads[u]])
        for t in tiles:
            ds[u, t, :] = (s[slot, u, t, :] * (dp[u, t, :] - dsum)).astype(BF16)
        acc[u] += dot_tn(key_ref[:, heads[u]], ds[u])
        key_term = dot_nn(ds[u], q[c, :, heads[u]]) * scale
        value_term = dot_nn(p[slot, u], do[c, :, heads[u]])
        return key_term, value_term

    def per_chunk(c, carry):
        b = lax.div(c, per)
        for u in range(GROUP):
            top[u] = jnp.full((1, rows), LOW, F32)
            norm[u] = jnp.zeros((1, rows), F32)
            scores = dot_nt(kv[c, 0, :, heads[u]], q[c, :, heads[u]])
            s[levels, u] = scores
        for u in range(GROUP):
            for t in tiles:
                at = lax.broadcasted_iota(jnp.int32, (TILE, rows), 0) + t.start
                to = lax.broadcasted_iota(jnp.int32, (TILE, rows), 1)
                s[levels, u, t, :] = jnp.where(at <= to, s[levels, u, t, :], LOW)
            absorb(levels, u)

        def score(j, carry):
            @pl.when(bit(j) == 1)
            def _():
                send_kv(j, c).wait_recv()
                for u in range(GROUP):
                    s[j, u] = dot_nt(far[j, c, 0, :, heads[u]], q[c, :, heads[u]])
                for u in range(GROUP):
                    absorb(j, u)
            return carry

        lax.fori_loop(0, levels, score, 0)

        @pl.when(lax.rem(c, per) == 0)
        def _():
            send_og(b).wait_recv()
        w_rows = pl.ds(pl.multiple_of(lax.rem(c, per) * width, width), width)
        do[c] = (
            dot_nt(og[b], w[w_rows, pl.ds(own_cols, half)])
            + dot_nt(og_far[b], w[w_rows, pl.ds(far_cols, half)])
        ).astype(BF16)

        for u in range(GROUP):
            norm[u] = top[u] * rate + jnp.log2(norm[u])
            acc[u] = jnp.zeros((HEAD_DIM, rows), F32)
        for u in range(GROUP):
            weigh(levels, u, kv.at[c, 1])

        def weighted(j, carry):
            @pl.when(bit(j) == 1)
            def _():
                for u in range(GROUP):
                    weigh(j, u, far.at[j, c, 1])
            return carry

        lax.fori_loop(0, levels, weighted, 0)

        for u in range(GROUP):
            mixed = acc[u].astype(BF16).astype(F32)
            lean = do[c, :, heads[u]].astype(F32).T
            norm[u] = jnp.sum(mixed * lean, axis=0, keepdims=True)
            at = pl.multiple_of(lax.rem(c, per) * width, width) + u * HEAD_DIM
            attn[b, :, pl.ds(pl.multiple_of(at, HEAD_DIM), HEAD_DIM)] = mixed.T.astype(BF16)
            acc[u] = jnp.zeros((HEAD_DIM, rows), F32)

        @pl.when(lax.rem(c, per) == per - 1)
        def _():
            for t in range(0, half, width):
                at = pl.ds(pl.multiple_of(far_cols + t, width), width)
                po[b, :, t:t + width] = dot_nn(attn[b], w[:, at]).astype(BF16)
            send_po(b).start()
            for t in range(0, half, width):
                at = pl.ds(pl.multiple_of(own_cols + t, width), width)
                lo[b, :, t:t + width] = dot_nn(attn[b], w[:, at])

        for u in range(GROUP):
            key_term, value_term = back(levels, u, c, kv.at[c, 0], kv.at[c, 1])
            own[c, 0, :, heads[u]] = key_term
            own[c, 1, :, heads[u]] = value_term

        def backward(j, carry):
            @pl.when(bit(j) == 1)
            def _():
                for u in range(GROUP):
                    key_term, value_term = back(j, u, c, far.at[j, c, 0], far.at[j, c, 1])
                    far[j, c, 0, :, heads[u]] = key_term.astype(BF16)
                    far[j, c, 1, :, heads[u]] = value_term.astype(BF16)
            return carry

        lax.fori_loop(0, levels, backward, 0)
        for u in range(GROUP):
            dq[c, :, heads[u]] = (acc[u] * scale).T.astype(BF16)
        put_dq(c).start()
        for j in range(levels):
            @pl.when(bit(j) == 1)
            def _():
                send_grad(j, c).start()
        return carry

    lax.fori_loop(0, chunks, per_chunk, 0)

    def finish(c, carry):
        for j in range(levels):
            @pl.when(bit(j) == 0)
            def _():
                send_kv(j, c).wait_send()
                send_grad(j, c).wait_recv()
                for i in range(2):
                    for t in tiles:
                        own[c, i, t, :] += far[j, c, i, t, :].astype(F32)
        for i in range(2):
            for t in tiles:
                kv[c, i, t, :] = own[c, i, t, :].astype(BF16)
            put_grad(c, i).start()
        return carry

    lax.fori_loop(0, chunks, finish, 0)

    outs = []
    for b in range(batch):
        send_po(b).wait_recv()
        send_og(b).wait_send()
        for t in tiles:
            og[b, t, :] = (lo[b, t, :] + po_far[b, t, :].astype(F32)).astype(BF16)
        copy = pltpu.make_async_copy(og.at[b], lo_out.at[b], ld_og.at[b])
        copy.start()
        outs.append(copy)

    def drain(c, carry):
        put_dq(c).wait()
        put_grad(c, 0).wait()
        put_grad(c, 1).wait()
        for j in range(levels):
            @pl.when(bit(j) == 1)
            def _():
                send_grad(j, c).wait_send()
        return carry

    lax.fori_loop(0, chunks, drain, 0)
    for b in range(batch):
        send_po(b).wait_send()
        outs[b].wait()


def solution(mesh):
    levels = mesh.shape["seq"].bit_length() - 1

    def step(queries, key_states, value_states, output_grad, out_proj):
        batch, rows, half = queries.shape
        width = GROUP * HEAD_DIM
        chunks = batch * (half // width)
        shape = jax.ShapeDtypeStruct(queries.shape, BF16)
        hbm = pl.BlockSpec(memory_space=pl.ANY)
        dma = pltpu.SemaphoreType.DMA
        return tuple(pl.pallas_call(
            functools.partial(kernel, levels),
            name="butterfly",
            out_shape=[shape] * 4,
            in_specs=[hbm] * 5,
            out_specs=[hbm] * 4,
            scratch_shapes=[
                pltpu.VMEM((chunks, rows, width), BF16),
                pltpu.VMEM((chunks, 2, rows, width), BF16),
                pltpu.VMEM((levels, chunks, 2, rows, width), BF16),
                pltpu.VMEM((chunks, rows, width), BF16),
                pltpu.VMEM(out_proj.shape, BF16),
                pltpu.VMEM((batch, rows, half), BF16),
                pltpu.VMEM((batch, rows, half), BF16),
                pltpu.VMEM((batch, rows, half), BF16),
                pltpu.VMEM((levels + 1, GROUP, rows, rows), F32),
                pltpu.VMEM((levels + 1, GROUP, rows, rows), BF16),
                pltpu.VMEM((GROUP, rows, rows), F32),
                pltpu.VMEM((GROUP, rows, rows), BF16),
                pltpu.VMEM((GROUP, 1, rows), F32),
                pltpu.VMEM((GROUP, 1, rows), F32),
                pltpu.VMEM((GROUP, HEAD_DIM, rows), F32),
                pltpu.VMEM((chunks, 2, rows, width), F32),
                pltpu.VMEM((chunks, rows, width), BF16),
                pltpu.VMEM((batch, rows, half), BF16),
                pltpu.VMEM((batch, rows, half), BF16),
                pltpu.VMEM((batch, rows, half), F32),
                dma((chunks,)),
                dma((chunks, 2)),
                dma((batch,)),
                dma,
                dma((batch,)),
                dma((batch,)),
                dma((batch,)),
                dma((batch,)),
                dma((levels, chunks)),
                dma((levels, chunks)),
                dma((chunks,)),
                dma((chunks, 2)),
            ],
            compiler_params=pltpu.CompilerParams(
                collective_id=0, has_side_effects=True, vmem_limit_bytes=60 << 20
            ),
        )(queries, key_states, value_states, output_grad, out_proj))

    act = P(None, "seq", "head")
    return jax.shard_map(
        step, mesh=mesh, in_specs=(act, act, act, act, P("head", None)),
        out_specs=(act,) * 4, check_vma=False,
    )
```

```python
import functools
import math

import jax
import jax.numpy as jnp
from jax import lax
from jax.experimental import pallas as pl
from jax.experimental.pallas import tpu as pltpu
from jax.sharding import PartitionSpec as P

HEAD_DIM = 128
GROUP = 2
MESH = pl.DeviceIdType.MESH
F32 = jnp.float32
BF16 = jnp.bfloat16
LOW = -1e30
TILE = 32
AHEAD = 3
LAG = 2


def dot_nt(a, b):
    return lax.dot_general(a, b, (((1,), (1,)), ((), ())), preferred_element_type=F32)


def dot_nn(a, b):
    return lax.dot_general(a, b, (((1,), (0,)), ((), ())), preferred_element_type=F32)


def dot_tn(a, b):
    return lax.dot_general(a, b, (((0,), (0,)), ((), ())), preferred_element_type=F32)


def kernel(
    levels, q_in, k_in, v_in, og_in, w_in, lo_out, dq_out, dk_out, dv_out,
    kv, qd, far, w, og, og_far, attn, s, p, dp, ds, top, norm, acc, own, dq, po, po_far, lo, st, st_far,
    ld_q, ld_kv, ld_og, ld_w, og_send, og_recv, po_send, po_recv,
    kv_send, kv_recv, do_send, do_recv, st_send, st_recv, out_sem, grad_sem,
):
    me = lax.axis_index("seq")
    hd = lax.axis_index("head")
    chunks, _, rows, width = kv.shape
    batch = og.shape[0]
    half = og.shape[2]
    per = chunks // batch
    scale = HEAD_DIM ** -0.5
    rate = scale * math.log2(math.e)
    own_cols = pl.multiple_of(hd * half, half)
    far_cols = pl.multiple_of((1 - hd) * half, half)

    def bit(j):
        return lax.rem(lax.shift_right_logical(me, j), 2)

    def partner(j):
        return me + (1 - 2 * bit(j)) * (1 << j)

    def cols(c):
        return pl.ds(pl.multiple_of(lax.rem(c, per) * width, width), width)

    def load_kv(c, i):
        src = (k_in, v_in)[i].at[lax.div(c, per), :, cols(c)]
        return pltpu.make_async_copy(src, kv.at[c, i], ld_kv.at[c, i])

    def load_q(c):
        return pltpu.make_async_copy(q_in.at[lax.div(c, per), :, cols(c)], qd.at[c, 0], ld_q.at[c])

    def load_og(b):
        return pltpu.make_async_copy(og_in.at[b], og.at[b], ld_og.at[b])

    load_w = pltpu.make_async_copy(w_in, w, ld_w)

    def to_head(src, dst, send, recv):
        return pltpu.make_async_remote_copy(
            src, dst, send, recv, device_id=(me, 1 - hd), device_id_type=MESH)

    def to_partner(j, src, dst, send, recv):
        return pltpu.make_async_remote_copy(
            src, dst, send, recv, device_id=(partner(j), hd), device_id_type=MESH)

    def send_og(b):
        return to_head(og_in.at[b], og_far.at[b], og_send.at[b], og_recv.at[b])

    def send_po(b):
        return to_head(po.at[b], po_far.at[b], po_send.at[b], po_recv.at[b])

    def send_kv(j, c):
        return to_partner(j, kv.at[c], far.at[j, c], kv_send.at[j, c], kv_recv.at[j, c])

    def send_q(j, c):
        return to_partner(j, qd.at[c, 0], far.at[j, c, 0], kv_send.at[j, c], kv_recv.at[j, c])

    def send_do(j, c):
        return to_partner(j, qd.at[c, 1], far.at[j, c, 1], do_send.at[j, c], do_recv.at[j, c])

    def send_st(j, c):
        return to_partner(j, st.at[c], st_far.at[j, c], st_send.at[j, c], st_recv.at[j, c])

    def put_dq(c):
        return pltpu.make_async_copy(dq.at[c], dq_out.at[lax.div(c, per), :, cols(c)], out_sem.at[c])

    def put_grad(c, i):
        dst = (dk_out, dv_out)[i].at[lax.div(c, per), :, cols(c)]
        return pltpu.make_async_copy(kv.at[c, i], dst, grad_sem.at[c, i])

    def start_loads(c, carry):
        load_kv(c, 0).start()
        load_kv(c, 1).start()
        load_q(c).start()
        return carry

    lax.fori_loop(0, chunks, start_loads, 0)
    for b in range(batch):
        load_og(b).start()
    load_w.start()

    barrier = pltpu.get_barrier_semaphore()
    for j in range(levels):
        pl.semaphore_signal(barrier, inc=1, device_id=(partner(j), hd), device_id_type=MESH)
    pl.semaphore_signal(barrier, inc=1, device_id=(me, 1 - hd), device_id_type=MESH)
    st[...] = jnp.zeros_like(st)
    pl.semaphore_wait(barrier, levels + 1)

    heads = [slice(u * HEAD_DIM, (u + 1) * HEAD_DIM) for u in range(GROUP)]
    tiles = [slice(t, t + TILE) for t in range(0, rows, TILE)]

    def issue(c):
        load_kv(c, 0).wait()
        load_kv(c, 1).wait()
        load_q(c).wait()
        for j in range(levels):
            @pl.when(bit(j) == 0)
            def _():
                send_kv(j, c).start()

            @pl.when(bit(j) == 1)
            def _():
                send_q(j, c).start()

    def issue_do(c):
        b = lax.div(c, per)

        @pl.when(lax.rem(c, per) == 0)
        def _():
            send_og(b).wait_recv()

        w_rows = pl.ds(pl.multiple_of(lax.rem(c, per) * width, width), width)
        qd[c, 1] = (
            dot_nt(og[b], w[w_rows, pl.ds(own_cols, half)])
            + dot_nt(og_far[b], w[w_rows, pl.ds(far_cols, half)])
        ).astype(BF16)
        for j in range(levels):
            @pl.when(bit(j) == 1)
            def _():
                send_do(j, c).start()

    send_og(0).start()

    def start_sends(c, carry):
        issue(c)
        if batch > 1:
            @pl.when(c == min(1, AHEAD - 1))
            def _():
                for b in range(1, batch):
                    send_og(b).start()
        return carry

    lax.fori_loop(0, AHEAD, start_sends, 0)
    for b in range(batch):
        load_og(b).wait()
    load_w.wait()
    lax.fori_loop(0, AHEAD, lambda c, carry: (issue_do(c), carry)[1], 0)

    def absorb(slot, u):
        peak = s[slot, u, tiles[0], :]
        for t in tiles[1:]:
            peak = jnp.maximum(peak, s[slot, u, t, :])
        old = top[u]
        new = jnp.maximum(old, jnp.max(peak, axis=0, keepdims=True))
        total = None
        for t in tiles:
            e = jnp.exp2((s[slot, u, t, :] - new) * rate)
            total = e if total is None else total + e
        norm[u] = norm[u] * jnp.exp2((old - new) * rate) + jnp.sum(total, axis=0, keepdims=True)
        top[u] = new

    def weigh(slot, u, c, value_ref):
        shift = norm[u]
        dp[slot, u] = dot_nt(value_ref[:, heads[u]], qd[c, 1, :, heads[u]])
        for t in tiles:
            e = jnp.exp2(s[slot, u, t, :] * rate - shift)
            s[slot, u, t, :] = e
            p[slot, u, t, :] = e.astype(BF16)
        acc[u] += dot_tn(value_ref[:, heads[u]], p[slot, u])

    def back(slot, u, key_ref):
        dsum = norm[u]
        for t in tiles:
            ds[u, t, :] = (s[slot, u, t, :] * (dp[slot, u, t, :] - dsum)).astype(BF16)
        acc[u] += dot_tn(key_ref[:, heads[u]], ds[u])

    def lower(c):
        k = lax.rem(c, LAG + 1)

        def one(j, carry):
            @pl.when(bit(j) == 0)
            def _():
                send_q(j, c).wait_recv()
                send_do(j, c).wait_recv()
                send_st(j, c).wait_recv()
                for u in range(GROUP):
                    s[j, u] = dot_nt(kv[c, 0, :, heads[u]], far[j, c, 0, :, heads[u]])
                    dp[j, u] = dot_nt(kv[c, 1, :, heads[u]], far[j, c, 1, :, heads[u]])
                for u in range(GROUP):
                    shift = st_far[j, c, u:u + 1, :]
                    dsum = st_far[j, c, GROUP + u:GROUP + u + 1, :]
                    for t in tiles:
                        e = jnp.exp2(s[j, u, t, :] * rate - shift)
                        p[j, u, t, :] = e.astype(BF16)
                        ds[u, t, :] = (e * (dp[j, u, t, :] - dsum)).astype(BF16)
                    own[k, 1, :, heads[u]] += dot_nn(p[j, u], far[j, c, 1, :, heads[u]])
                    own[k, 0, :, heads[u]] += dot_nn(ds[u], far[j, c, 0, :, heads[u]])
            return carry

        lax.fori_loop(0, levels, one, 0)
        for j in range(levels):
            @pl.when(bit(j) == 0)
            def _():
                send_kv(j, c).wait_send()
        for t in tiles:
            kv[c, 0, t, :] = (own[k, 0, t, :] * scale).astype(BF16)
            kv[c, 1, t, :] = own[k, 1, t, :].astype(BF16)
        for i in range(2):
            put_grad(c, i).start()

    def per_chunk(c, carry):
        b = lax.div(c, per)
        k = lax.rem(c, LAG + 1)
        for u in range(GROUP):
            top[u] = jnp.full((1, rows), LOW, F32)
            norm[u] = jnp.zeros((1, rows), F32)
            s[levels, u] = dot_nt(kv[c, 0, :, heads[u]], qd[c, 0, :, heads[u]])
        for u in range(GROUP):
            for t in tiles:
                at = lax.broadcasted_iota(jnp.int32, (TILE, rows), 0) + t.start
                to = lax.broadcasted_iota(jnp.int32, (TILE, rows), 1)
                s[levels, u, t, :] = jnp.where(at <= to, s[levels, u, t, :], LOW)
            absorb(levels, u)

        def score(j, carry):
            @pl.when(bit(j) == 1)
            def _():
                send_kv(j, c).wait_recv()
                for u in range(GROUP):
                    s[j, u] = dot_nt(far[j, c, 0, :, heads[u]], qd[c, 0, :, heads[u]])
                for u in range(GROUP):
                    absorb(j, u)
            return carry

        lax.fori_loop(0, levels, score, 0)

        for u in range(GROUP):
            norm[u] = top[u] * rate + jnp.log2(norm[u])
            st[c, u:u + 1, :] = norm[u]
            acc[u] = jnp.zeros((HEAD_DIM, rows), F32)
        for u in range(GROUP):
            weigh(levels, u, c, kv.at[c, 1])

        def weighted(j, carry):
            @pl.when(bit(j) == 1)
            def _():
                for u in range(GROUP):
                    weigh(j, u, c, far.at[j, c, 1])
            return carry

        lax.fori_loop(0, levels, weighted, 0)

        for u in range(GROUP):
            mixed = acc[u].astype(BF16).astype(F32)
            lean = qd[c, 1, :, heads[u]].astype(F32).T
            norm[u] = jnp.sum(mixed * lean, axis=0, keepdims=True)
            st[c, GROUP + u:GROUP + u + 1, :] = norm[u]
            at = pl.multiple_of(lax.rem(c, per) * width, width) + u * HEAD_DIM
            attn[b, :, pl.ds(pl.multiple_of(at, HEAD_DIM), HEAD_DIM)] = mixed.T.astype(BF16)
            acc[u] = jnp.zeros((HEAD_DIM, rows), F32)
        for j in range(levels):
            @pl.when(bit(j) == 1)
            def _():
                send_st(j, c).start()

        @pl.when(c + AHEAD < chunks)
        def _():
            issue(c + AHEAD)
            issue_do(c + AHEAD)

        @pl.when(lax.rem(c, per) == per - 1)
        def _():
            for t in range(0, half, width):
                at = pl.ds(pl.multiple_of(far_cols + t, width), width)
                po[b, :, t:t + width] = dot_nn(attn[b], w[:, at]).astype(BF16)
            send_po(b).start()
            for t in range(0, half, width):
                at = pl.ds(pl.multiple_of(own_cols + t, width), width)
                lo[b, :, t:t + width] = dot_nn(attn[b], w[:, at])

        for u in range(GROUP):
            back(levels, u, kv.at[c, 0])
            own[k, 0, :, heads[u]] = dot_nn(ds[u], qd[c, 0, :, heads[u]])
            own[k, 1, :, heads[u]] = dot_nn(p[levels, u], qd[c, 1, :, heads[u]])

        def backward(j, carry):
            @pl.when(bit(j) == 1)
            def _():
                for u in range(GROUP):
                    back(j, u, far.at[j, c, 0])
            return carry

        lax.fori_loop(0, levels, backward, 0)
        for u in range(GROUP):
            dq[c, :, heads[u]] = (acc[u] * scale).T.astype(BF16)
        put_dq(c).start()

        @pl.when(c >= LAG)
        def _():
            lower(c - LAG)
        return carry

    lax.fori_loop(0, chunks, per_chunk, 0)
    lax.fori_loop(chunks - LAG, chunks, lambda c, carry: (lower(c), carry)[1], 0)

    outs = []
    for b in range(batch):
        send_po(b).wait_recv()
        send_og(b).wait_send()
        for t in tiles:
            og[b, t, :] = (lo[b, t, :] + po_far[b, t, :].astype(F32)).astype(BF16)
        copy = pltpu.make_async_copy(og.at[b], lo_out.at[b], ld_og.at[b])
        copy.start()
        outs.append(copy)

    def drain(c, carry):
        put_dq(c).wait()
        put_grad(c, 0).wait()
        put_grad(c, 1).wait()
        for j in range(levels):
            @pl.when(bit(j) == 1)
            def _():
                send_q(j, c).wait_send()
                send_do(j, c).wait_send()
                send_st(j, c).wait_send()
        return carry

    lax.fori_loop(0, chunks, drain, 0)
    for b in range(batch):
        send_po(b).wait_send()
        outs[b].wait()


def solution(mesh):
    levels = mesh.shape["seq"].bit_length() - 1

    def step(queries, key_states, value_states, output_grad, out_proj):
        batch, rows, half = queries.shape
        width = GROUP * HEAD_DIM
        chunks = batch * (half // width)
        shape = jax.ShapeDtypeStruct(queries.shape, BF16)
        hbm = pl.BlockSpec(memory_space=pl.ANY)
        dma = pltpu.SemaphoreType.DMA
        return tuple(pl.pallas_call(
            functools.partial(kernel, levels),
            name="butterfly",
            out_shape=[shape] * 4,
            in_specs=[hbm] * 5,
            out_specs=[hbm] * 4,
            scratch_shapes=[
                pltpu.VMEM((chunks, 2, rows, width), BF16),
                pltpu.VMEM((chunks, 2, rows, width), BF16),
                pltpu.VMEM((levels, chunks, 2, rows, width), BF16),
                pltpu.VMEM(out_proj.shape, BF16),
                pltpu.VMEM((batch, rows, half), BF16),
                pltpu.VMEM((batch, rows, half), BF16),
                pltpu.VMEM((batch, rows, half), BF16),
                pltpu.VMEM((levels + 1, GROUP, rows, rows), F32),
                pltpu.VMEM((levels + 1, GROUP, rows, rows), BF16),
                pltpu.VMEM((levels + 1, GROUP, rows, rows), F32),
                pltpu.VMEM((GROUP, rows, rows), BF16),
                pltpu.VMEM((GROUP, 1, rows), F32),
                pltpu.VMEM((GROUP, 1, rows), F32),
                pltpu.VMEM((GROUP, HEAD_DIM, rows), F32),
                pltpu.VMEM((LAG + 1, 2, rows, width), F32),
                pltpu.VMEM((chunks, rows, width), BF16),
                pltpu.VMEM((batch, rows, half), BF16),
                pltpu.VMEM((batch, rows, half), BF16),
                pltpu.VMEM((batch, rows, half), F32),
                pltpu.VMEM((chunks, 8, rows), F32),
                pltpu.VMEM((levels, chunks, 8, rows), F32),
                dma((chunks,)),
                dma((chunks, 2)),
                dma((batch,)),
                dma,
                dma((batch,)),
                dma((batch,)),
                dma((batch,)),
                dma((batch,)),
                dma((levels, chunks)),
                dma((levels, chunks)),
                dma((levels, chunks)),
                dma((levels, chunks)),
                dma((levels, chunks)),
                dma((levels, chunks)),
                dma((chunks,)),
                dma((chunks, 2)),
            ],
            compiler_params=pltpu.CompilerParams(
                collective_id=0, has_side_effects=True, vmem_limit_bytes=60 << 20
            ),
        )(queries, key_states, value_states, output_grad, out_proj))

    act = P(None, "seq", "head")
    return jax.shard_map(
        step, mesh=mesh, in_specs=(act, act, act, act, P("head", None)),
        out_specs=(act,) * 4, check_vma=False,
    )
```

```python
import functools
import math

import jax
import jax.numpy as jnp
from jax import lax
from jax.experimental import pallas as pl
from jax.experimental.pallas import tpu as pltpu
from jax.sharding import PartitionSpec as P

HEAD_DIM = 128
GROUP = 2
MESH = pl.DeviceIdType.MESH
F32 = jnp.float32
BF16 = jnp.bfloat16
LOW = -1e30
TILE = 32
RINGS = ((2, 3), (4, 5))
AHEAD = 2
AHEAD_KV = 8
OG_AT = 1
LAG = 3


def dot_nt(a, b):
    return lax.dot_general(a, b, (((1,), (1,)), ((), ())), preferred_element_type=F32)


def dot_nn(a, b):
    return lax.dot_general(a, b, (((1,), (0,)), ((), ())), preferred_element_type=F32)


def dot_tn(a, b):
    return lax.dot_general(a, b, (((0,), (0,)), ((), ())), preferred_element_type=F32)


def kernel(
    levels, q_in, k_in, v_in, og_in, w_in, lo_out, dq_out, dk_out, dv_out,
    kv, qd, far, w, og, og_far, attn, s, p, dp, ds, top, norm, acc, own, po, po_far, lo, st, st_far,
    ld_q, ld_kv, ld_og, ld_w, og_send, og_recv, po_send, po_recv,
    kv_send, kv_recv, do_send, do_recv, st_send, st_recv, pass_send,
):
    me = lax.axis_index("seq")
    hd = lax.axis_index("head")
    chunks, _, rows, width = kv.shape
    batch = og.shape[0]
    half = og.shape[2]
    per = chunks // batch
    scale = HEAD_DIM ** -0.5
    rate = scale * math.log2(math.e)
    own_cols = pl.multiple_of(hd * half, half)
    far_cols = pl.multiple_of((1 - hd) * half, half)

    def bit(j):
        return lax.rem(lax.shift_right_logical(me, j), 2)

    def partner(j):
        return me + (1 - 2 * bit(j)) * (1 << j)

    def cols(c):
        return pl.ds(pl.multiple_of(lax.rem(c, per) * width, width), width)

    def load_kv(c, i):
        src = (k_in, v_in)[i].at[lax.div(c, per), :, cols(c)]
        return pltpu.make_async_copy(src, kv.at[c, i], ld_kv.at[c, i])

    def load_q(c):
        return pltpu.make_async_copy(q_in.at[lax.div(c, per), :, cols(c)], qd.at[c, 0], ld_q.at[c])

    def load_og(b):
        return pltpu.make_async_copy(og_in.at[b], og.at[b], ld_og.at[b])

    load_w = pltpu.make_async_copy(w_in, w, ld_w)

    def to_head(src, dst, send, recv):
        return pltpu.make_async_remote_copy(
            src, dst, send, recv, device_id=(me, 1 - hd), device_id_type=MESH)

    def to_partner(j, src, dst, send, recv):
        return pltpu.make_async_remote_copy(
            src, dst, send, recv, device_id=(partner(j), hd), device_id_type=MESH)

    def send_og(b):
        return to_head(og_in.at[b], og_far.at[b], og_send.at[b], og_recv.at[b])

    def send_po(b):
        return to_head(po.at[b], po_far.at[b], po_send.at[b], po_recv.at[b])

    def send_kv(j, c):
        return to_partner(j, kv.at[c], far.at[j, c], kv_send.at[j, c], kv_recv.at[j, c])

    def passes(ring):
        near, apart = RINGS[ring]
        return (bit(near) == 1) & (bit(apart) == 0)

    def opposite(ring):
        near, apart = RINGS[ring]
        return partner(near) + partner(apart) - me

    def pass_kv(ring, c):
        near, apart = RINGS[ring]
        return pltpu.make_async_remote_copy(
            far.at[near, c], far.at[apart, c], pass_send.at[ring, c], kv_recv.at[apart, c],
            device_id=(opposite(ring), hd), device_id_type=MESH)

    def pass_on(c):
        for ring in range(len(RINGS)):
            @pl.when(passes(ring))
            def _():
                send_kv(RINGS[ring][0], c).wait_recv()
                pass_kv(ring, c).start()

    def sends_own(j):
        sender = bit(j) == 0
        for near, apart in RINGS:
            if j == apart:
                sender = sender & (bit(near) == 1)
        return sender

    def send_q(j, c):
        return to_partner(j, qd.at[c, 0], far.at[j, c, 0], kv_send.at[j, c], kv_recv.at[j, c])

    def send_do(j, c):
        return to_partner(j, qd.at[c, 1], far.at[j, c, 1], do_send.at[j, c], do_recv.at[j, c])

    def send_st(j, c):
        return to_partner(j, st.at[c], st_far.at[j, c], st_send.at[j, c], st_recv.at[j, c])

    def start_loads(c, carry):
        load_kv(c, 0).start()
        load_kv(c, 1).start()
        load_q(c).start()
        return carry

    lax.fori_loop(0, chunks, start_loads, 0)
    for b in range(batch):
        load_og(b).start()
    load_w.start()

    barrier = pltpu.get_barrier_semaphore()
    for j in range(levels):
        pl.semaphore_signal(barrier, inc=1, device_id=(partner(j), hd), device_id_type=MESH)
    for ring in range(len(RINGS)):
        pl.semaphore_signal(barrier, inc=1, device_id=(opposite(ring), hd), device_id_type=MESH)
    pl.semaphore_signal(barrier, inc=1, device_id=(me, 1 - hd), device_id_type=MESH)
    st[...] = jnp.zeros_like(st)
    pl.semaphore_wait(barrier, levels + 1 + len(RINGS))

    heads = [slice(u * HEAD_DIM, (u + 1) * HEAD_DIM) for u in range(GROUP)]
    tiles = [slice(t, t + TILE) for t in range(0, rows, TILE)]

    def issue_kv(c):
        load_kv(c, 0).wait()
        load_kv(c, 1).wait()
        for j in range(levels):
            @pl.when(sends_own(j))
            def _():
                send_kv(j, c).start()

    def issue(c):
        load_q(c).wait()
        for j in range(levels):
            @pl.when(bit(j) == 1)
            def _():
                send_q(j, c).start()

    def issue_do(c):
        b = lax.div(c, per)

        @pl.when(lax.rem(c, per) == 0)
        def _():
            send_og(b).wait_recv()

        w_rows = pl.ds(pl.multiple_of(lax.rem(c, per) * width, width), width)
        qd[c, 1] = (
            dot_nt(og[b], w[w_rows, pl.ds(own_cols, half)])
            + dot_nt(og_far[b], w[w_rows, pl.ds(far_cols, half)])
        ).astype(BF16)
        for j in range(levels):
            @pl.when(bit(j) == 1)
            def _():
                send_do(j, c).start()

    send_og(0).start()

    def start_sends(c, carry):
        issue_kv(c)

        @pl.when(c < AHEAD)
        def _():
            issue(c)
        if batch > 1:
            @pl.when(c == OG_AT)
            def _():
                for b in range(1, batch):
                    send_og(b).start()
        return carry

    lax.fori_loop(0, AHEAD_KV, start_sends, 0)
    for b in range(batch):
        load_og(b).wait()
    load_w.wait()
    lax.fori_loop(0, AHEAD, lambda c, carry: (issue_do(c), carry)[1], 0)

    def absorb(slot, u):
        peak = s[slot, u, tiles[0], :]
        for t in tiles[1:]:
            peak = jnp.maximum(peak, s[slot, u, t, :])
        old = top[u]
        new = jnp.maximum(old, jnp.max(peak, axis=0, keepdims=True))
        total = None
        for t in tiles:
            e = jnp.exp2((s[slot, u, t, :] - new) * rate)
            total = e if total is None else total + e
        norm[u] = norm[u] * jnp.exp2((old - new) * rate) + jnp.sum(total, axis=0, keepdims=True)
        top[u] = new

    def weigh(slot, u, c, value_ref):
        shift = norm[u]
        dp[slot, u] = dot_nt(value_ref[:, heads[u]], qd[c, 1, :, heads[u]])
        for t in tiles:
            e = jnp.exp2(s[slot, u, t, :] * rate - shift)
            s[slot, u, t, :] = e
            p[slot, u, t, :] = e.astype(BF16)
        acc[u] += dot_tn(value_ref[:, heads[u]], p[slot, u])

    def back(slot, u, key_ref):
        dsum = norm[u]
        for t in tiles:
            ds[u, t, :] = (s[slot, u, t, :] * (dp[slot, u, t, :] - dsum)).astype(BF16)
        acc[u] += dot_tn(key_ref[:, heads[u]], ds[u])

    def lower(c):
        b = lax.div(c, per)
        k = lax.rem(c, LAG + 1)

        def one(j, carry):
            @pl.when(bit(j) == 0)
            def _():
                send_q(j, c).wait_recv()
                send_do(j, c).wait_recv()
                send_st(j, c).wait_recv()
                for u in range(GROUP):
                    s[j, u] = dot_nt(kv[c, 0, :, heads[u]], far[j, c, 0, :, heads[u]])
                    dp[j, u] = dot_nt(kv[c, 1, :, heads[u]], far[j, c, 1, :, heads[u]])
                for u in range(GROUP):
                    shift = st_far[j, c, u:u + 1, :]
                    dsum = st_far[j, c, GROUP + u:GROUP + u + 1, :]
                    for t in tiles:
                        e = jnp.exp2(s[j, u, t, :] * rate - shift)
                        p[j, u, t, :] = e.astype(BF16)
                        ds[u, t, :] = (e * (dp[j, u, t, :] - dsum)).astype(BF16)
                    own[k, 1, :, heads[u]] += dot_nn(p[j, u], far[j, c, 1, :, heads[u]])
                    own[k, 0, :, heads[u]] += dot_nn(ds[u], far[j, c, 0, :, heads[u]])
            return carry

        lax.fori_loop(0, levels, one, 0)
        for t in tiles:
            dk_out[b, t, cols(c)] = (own[k, 0, t, :] * scale).astype(BF16)
            dv_out[b, t, cols(c)] = own[k, 1, t, :].astype(BF16)

    def per_chunk(c, carry):
        b = lax.div(c, per)
        k = lax.rem(c, LAG + 1)
        for u in range(GROUP):
            top[u] = jnp.full((1, rows), LOW, F32)
            norm[u] = jnp.zeros((1, rows), F32)
            s[levels, u] = dot_nt(kv[c, 0, :, heads[u]], qd[c, 0, :, heads[u]])
        for u in range(GROUP):
            for t in tiles:
                at = lax.broadcasted_iota(jnp.int32, (TILE, rows), 0) + t.start
                to = lax.broadcasted_iota(jnp.int32, (TILE, rows), 1)
                s[levels, u, t, :] = jnp.where(at <= to, s[levels, u, t, :], LOW)
            absorb(levels, u)

        def score(j, carry):
            held = False
            for ring in range(len(RINGS)):
                held = held | (passes(ring) & (j == RINGS[ring][0]))

            @pl.when((bit(j) == 1) & jnp.logical_not(held))
            def _():
                send_kv(j, c).wait_recv()

            @pl.when(bit(j) == 1)
            def _():
                for u in range(GROUP):
                    s[j, u] = dot_nt(far[j, c, 0, :, heads[u]], qd[c, 0, :, heads[u]])
                for u in range(GROUP):
                    absorb(j, u)
            return carry

        lax.fori_loop(0, levels, score, 0)

        @pl.when(c + 1 < chunks)
        def _():
            pass_on(c + 1)

        for u in range(GROUP):
            norm[u] = top[u] * rate + jnp.log2(norm[u])
            st[c, u:u + 1, :] = norm[u]
            acc[u] = jnp.zeros((HEAD_DIM, rows), F32)
        for u in range(GROUP):
            weigh(levels, u, c, kv.at[c, 1])

        def weighted(j, carry):
            @pl.when(bit(j) == 1)
            def _():
                for u in range(GROUP):
                    weigh(j, u, c, far.at[j, c, 1])
            return carry

        lax.fori_loop(0, levels, weighted, 0)

        for u in range(GROUP):
            mixed = acc[u].astype(BF16).astype(F32)
            lean = qd[c, 1, :, heads[u]].astype(F32).T
            norm[u] = jnp.sum(mixed * lean, axis=0, keepdims=True)
            st[c, GROUP + u:GROUP + u + 1, :] = norm[u]
            at = pl.multiple_of(lax.rem(c, per) * width, width) + u * HEAD_DIM
            attn[b, :, pl.ds(pl.multiple_of(at, HEAD_DIM), HEAD_DIM)] = mixed.T.astype(BF16)
            acc[u] = jnp.zeros((HEAD_DIM, rows), F32)
        for j in range(levels):
            @pl.when(bit(j) == 1)
            def _():
                send_st(j, c).start()

        @pl.when(c + AHEAD < chunks)
        def _():
            issue(c + AHEAD)
            issue_do(c + AHEAD)

        @pl.when(lax.rem(c, per) == per - 1)
        def _():
            for t in range(0, half, width):
                at = pl.ds(pl.multiple_of(far_cols + t, width), width)
                po[b, :, t:t + width] = dot_nn(attn[b], w[:, at]).astype(BF16)
            send_po(b).start()
            for t in range(0, half, width):
                at = pl.ds(pl.multiple_of(own_cols + t, width), width)
                lo[b, :, t:t + width] = dot_nn(attn[b], w[:, at])

        for u in range(GROUP):
            back(levels, u, kv.at[c, 0])
            own[k, 0, :, heads[u]] = dot_nn(ds[u], qd[c, 0, :, heads[u]])
            own[k, 1, :, heads[u]] = dot_nn(p[levels, u], qd[c, 1, :, heads[u]])

        def backward(j, carry):
            @pl.when(bit(j) == 1)
            def _():
                for u in range(GROUP):
                    back(j, u, far.at[j, c, 0])
            return carry

        lax.fori_loop(0, levels, backward, 0)
        for u in range(GROUP):
            at = pl.multiple_of(lax.rem(c, per) * width, width) + u * HEAD_DIM
            at = pl.ds(pl.multiple_of(at, HEAD_DIM), HEAD_DIM)
            dq_out[b, :, at] = (acc[u] * scale).T.astype(BF16)

        @pl.when(c >= LAG)
        def _():
            lower(c - LAG)
        return carry

    pass_on(0)
    lax.fori_loop(0, chunks, per_chunk, 0)
    lax.fori_loop(chunks - LAG, chunks, lambda c, carry: (lower(c), carry)[1], 0)

    for b in range(batch):
        send_po(b).wait_recv()
        for t in tiles:
            lo_out[b, t, :] = (lo[b, t, :] + po_far[b, t, :].astype(F32)).astype(BF16)

    def drain(c, carry):
        for j in range(levels):
            @pl.when(sends_own(j))
            def _():
                send_kv(j, c).wait_send()
        for ring in range(len(RINGS)):
            @pl.when(passes(ring))
            def _():
                pass_kv(ring, c).wait_send()
        for j in range(levels):
            @pl.when(bit(j) == 1)
            def _():
                send_q(j, c).wait_send()
                send_do(j, c).wait_send()
                send_st(j, c).wait_send()
        return carry

    lax.fori_loop(0, chunks, drain, 0)
    for b in range(batch):
        send_og(b).wait_send()
        send_po(b).wait_send()


def solution(mesh):
    levels = mesh.shape["seq"].bit_length() - 1

    def step(queries, key_states, value_states, output_grad, out_proj):
        batch, rows, half = queries.shape
        width = GROUP * HEAD_DIM
        chunks = batch * (half // width)
        shape = pltpu.VMEM(queries.shape, BF16)
        hbm = pl.BlockSpec(memory_space=pl.ANY)
        dma = pltpu.SemaphoreType.DMA
        return tuple(pl.pallas_call(
            functools.partial(kernel, levels),
            name="butterfly",
            out_shape=[shape] * 4,
            in_specs=[hbm] * 5,
            out_specs=[pl.BlockSpec(memory_space=pltpu.VMEM)] * 4,
            scratch_shapes=[
                pltpu.VMEM((chunks, 2, rows, width), BF16),
                pltpu.VMEM((chunks, 2, rows, width), BF16),
                pltpu.VMEM((levels, chunks, 2, rows, width), BF16),
                pltpu.VMEM(out_proj.shape, BF16),
                pltpu.VMEM((batch, rows, half), BF16),
                pltpu.VMEM((batch, rows, half), BF16),
                pltpu.VMEM((batch, rows, half), BF16),
                pltpu.VMEM((levels + 1, GROUP, rows, rows), F32),
                pltpu.VMEM((levels + 1, GROUP, rows, rows), BF16),
                pltpu.VMEM((levels + 1, GROUP, rows, rows), F32),
                pltpu.VMEM((GROUP, rows, rows), BF16),
                pltpu.VMEM((GROUP, 1, rows), F32),
                pltpu.VMEM((GROUP, 1, rows), F32),
                pltpu.VMEM((GROUP, HEAD_DIM, rows), F32),
                pltpu.VMEM((LAG + 1, 2, rows, width), F32),
                pltpu.VMEM((batch, rows, half), BF16),
                pltpu.VMEM((batch, rows, half), BF16),
                pltpu.VMEM((batch, rows, half), F32),
                pltpu.VMEM((chunks, 8, rows), F32),
                pltpu.VMEM((levels, chunks, 8, rows), F32),
                dma((chunks,)),
                dma((chunks, 2)),
                dma((batch,)),
                dma,
                dma((batch,)),
                dma((batch,)),
                dma((batch,)),
                dma((batch,)),
                dma((levels, chunks)),
                dma((levels, chunks)),
                dma((levels, chunks)),
                dma((levels, chunks)),
                dma((levels, chunks)),
                dma((levels, chunks)),
                dma((len(RINGS), chunks)),
            ],
            compiler_params=pltpu.CompilerParams(
                collective_id=0, has_side_effects=True, vmem_limit_bytes=119 << 19
            ),
        )(queries, key_states, value_states, output_grad, out_proj))

    act = P(None, "seq", "head")
    return jax.shard_map(
        step, mesh=mesh, in_specs=(act, act, act, act, P("head", None)),
        out_specs=(act,) * 4, check_vma=False,
    )
```

```python
import functools
import math

import jax
import jax.numpy as jnp
from jax import lax
from jax.experimental import pallas as pl
from jax.experimental.pallas import tpu as pltpu
from jax.sharding import PartitionSpec as P

HEAD_DIM = 128
GROUP = 2
MESH = pl.DeviceIdType.MESH
F32 = jnp.float32
BF16 = jnp.bfloat16
LOW = -1e30
TILE = 32
RINGS = ((2, 3), (4, 5))
AHEAD = 2
AHEAD_KV = 8
OG_AT = 1
LAG = 3


def dot_nt(a, b):
    return lax.dot_general(a, b, (((1,), (1,)), ((), ())), preferred_element_type=F32)


def dot_nn(a, b):
    return lax.dot_general(a, b, (((1,), (0,)), ((), ())), preferred_element_type=F32)


def dot_tn(a, b):
    return lax.dot_general(a, b, (((0,), (0,)), ((), ())), preferred_element_type=F32)


def kernel(
    levels, q_in, k_in, v_in, og_in, w_in, lo_out, dq_out, dk_out, dv_out,
    kv, qd, far, w, og, og_far, attn, s, p, dp, ds, top, norm, acc, own, po, po_far, lo, st, st_far,
    ld_q, ld_kv, ld_og, ld_w, og_send, og_recv, po_send, po_recv,
    kv_send, kv_recv, do_send, do_recv, st_send, st_recv, pass_send,
):
    me = lax.axis_index("seq")
    hd = lax.axis_index("head")
    chunks, _, rows, width = kv.shape
    batch = og.shape[0]
    half = og.shape[2]
    per = chunks // batch
    scale = HEAD_DIM ** -0.5
    rate = scale * math.log2(math.e)
    own_cols = pl.multiple_of(hd * half, half)
    far_cols = pl.multiple_of((1 - hd) * half, half)

    def bit(j):
        return lax.rem(lax.shift_right_logical(me, j), 2)

    def partner(j):
        return me + (1 - 2 * bit(j)) * (1 << j)

    def cols(c):
        return pl.ds(pl.multiple_of(lax.rem(c, per) * width, width), width)

    def load_kv(c, i):
        src = (k_in, v_in)[i].at[lax.div(c, per), :, cols(c)]
        return pltpu.make_async_copy(src, kv.at[c, i], ld_kv.at[c, i])

    def load_q(c):
        return pltpu.make_async_copy(q_in.at[lax.div(c, per), :, cols(c)], qd.at[c, 0], ld_q.at[c])

    def load_og(b):
        return pltpu.make_async_copy(og_in.at[b], og.at[b], ld_og.at[b])

    load_w = pltpu.make_async_copy(w_in, w, ld_w)

    def to_head(src, dst, send, recv):
        return pltpu.make_async_remote_copy(
            src, dst, send, recv, device_id=(me, 1 - hd), device_id_type=MESH)

    def to_partner(j, src, dst, send, recv):
        return pltpu.make_async_remote_copy(
            src, dst, send, recv, device_id=(partner(j), hd), device_id_type=MESH)

    def send_og(b):
        return to_head(og_in.at[b], og_far.at[b], og_send.at[b], og_recv.at[b])

    def send_po(b):
        return to_head(po.at[b], po_far.at[b], po_send.at[b], po_recv.at[b])

    def send_kv(j, c):
        return to_partner(j, kv.at[c], far.at[j, c], kv_send.at[j, c], kv_recv.at[j, c])

    def passes(ring):
        near, apart = RINGS[ring]
        return (bit(near) == 1) & (bit(apart) == 0)

    def opposite(ring):
        near, apart = RINGS[ring]
        return partner(near) + partner(apart) - me

    def pass_kv(ring, c):
        near, apart = RINGS[ring]
        return pltpu.make_async_remote_copy(
            far.at[near, c], far.at[apart, c], pass_send.at[ring, c], kv_recv.at[apart, c],
            device_id=(opposite(ring), hd), device_id_type=MESH)

    def pass_on(c):
        for ring in range(len(RINGS)):
            @pl.when(passes(ring))
            def _():
                send_kv(RINGS[ring][0], c).wait_recv()
                pass_kv(ring, c).start()

    def sends_own(j):
        sender = bit(j) == 0
        for near, apart in RINGS:
            if j == apart:
                sender = sender & (bit(near) == 1)
        return sender

    def send_q(j, c):
        return to_partner(j, qd.at[c, 0], far.at[j, c, 0], kv_send.at[j, c], kv_recv.at[j, c])

    def send_do(j, c):
        return to_partner(j, qd.at[c, 1], far.at[j, c, 1], do_send.at[j, c], do_recv.at[j, c])

    def send_st(j, c):
        return to_partner(j, st.at[c], st_far.at[j, c], st_send.at[j, c], st_recv.at[j, c])

    def start_loads(c, carry):
        load_kv(c, 0).start()
        load_kv(c, 1).start()
        load_q(c).start()
        return carry

    lax.fori_loop(0, chunks, start_loads, 0)
    for b in range(batch):
        load_og(b).start()
    load_w.start()

    barrier = pltpu.get_barrier_semaphore()
    for j in range(levels):
        pl.semaphore_signal(barrier, inc=1, device_id=(partner(j), hd), device_id_type=MESH)
    for ring in range(len(RINGS)):
        pl.semaphore_signal(barrier, inc=1, device_id=(opposite(ring), hd), device_id_type=MESH)
    pl.semaphore_signal(barrier, inc=1, device_id=(me, 1 - hd), device_id_type=MESH)
    st[...] = jnp.zeros_like(st)
    pl.semaphore_wait(barrier, levels + 1 + len(RINGS))

    heads = [slice(u * HEAD_DIM, (u + 1) * HEAD_DIM) for u in range(GROUP)]
    tiles = [slice(t, t + TILE) for t in range(0, rows, TILE)]

    def issue_kv(c):
        load_kv(c, 0).wait()
        load_kv(c, 1).wait()
        for j in range(levels):
            @pl.when(sends_own(j))
            def _():
                send_kv(j, c).start()

    def issue(c):
        load_q(c).wait()
        for j in range(levels):
            @pl.when(bit(j) == 1)
            def _():
                send_q(j, c).start()

    def issue_do(c):
        b = lax.div(c, per)

        @pl.when(lax.rem(c, per) == 0)
        def _():
            send_og(b).wait_recv()

        w_rows = pl.ds(pl.multiple_of(lax.rem(c, per) * width, width), width)
        qd[c, 1] = (
            dot_nt(og[b], w[w_rows, pl.ds(own_cols, half)])
            + dot_nt(og_far[b], w[w_rows, pl.ds(far_cols, half)])
        ).astype(BF16)
        for j in range(levels):
            @pl.when(bit(j) == 1)
            def _():
                send_do(j, c).start()

    send_og(0).start()

    def start_sends(c, carry):
        issue_kv(c)

        @pl.when(c < AHEAD)
        def _():
            issue(c)
        if batch > 1:
            @pl.when(c == OG_AT)
            def _():
                for b in range(1, batch):
                    send_og(b).start()
        return carry

    lax.fori_loop(0, AHEAD_KV, start_sends, 0)
    for b in range(batch):
        load_og(b).wait()
    load_w.wait()
    lax.fori_loop(0, AHEAD, lambda c, carry: (issue_do(c), carry)[1], 0)

    def absorb(slot, u):
        peak = s[slot, u, tiles[0], :]
        for t in tiles[1:]:
            peak = jnp.maximum(peak, s[slot, u, t, :])
        old = top[u]
        new = jnp.maximum(old, jnp.max(peak, axis=0, keepdims=True))
        total = None
        for t in tiles:
            e = jnp.exp2((s[slot, u, t, :] - new) * rate)
            total = e if total is None else total + e
        norm[u] = norm[u] * jnp.exp2((old - new) * rate) + jnp.sum(total, axis=0, keepdims=True)
        top[u] = new

    def weigh(slot, u, c, value_ref):
        shift = norm[u]
        dp[slot, u] = dot_nt(value_ref[:, heads[u]], qd[c, 1, :, heads[u]])
        for t in tiles:
            e = jnp.exp2(s[slot, u, t, :] * rate - shift)
            s[slot, u, t, :] = e
            p[slot, u, t, :] = e.astype(BF16)
        acc[u] += dot_tn(value_ref[:, heads[u]], p[slot, u])

    def back(slot, u, key_ref):
        dsum = norm[u]
        for t in tiles:
            ds[u, t, :] = (s[slot, u, t, :] * (dp[slot, u, t, :] - dsum)).astype(BF16)
        acc[u] += dot_tn(key_ref[:, heads[u]], ds[u])

    def lower(c):
        b = lax.div(c, per)
        k = lax.rem(c, LAG + 1)

        def one(j, carry):
            @pl.when(bit(j) == 0)
            def _():
                send_q(j, c).wait_recv()
                send_do(j, c).wait_recv()
                send_st(j, c).wait_recv()
                for u in range(GROUP):
                    s[j, u] = dot_nt(kv[c, 0, :, heads[u]], far[j, c, 0, :, heads[u]])
                    dp[j, u] = dot_nt(kv[c, 1, :, heads[u]], far[j, c, 1, :, heads[u]])
                for u in range(GROUP):
                    shift = st_far[j, c, u:u + 1, :]
                    dsum = st_far[j, c, GROUP + u:GROUP + u + 1, :]
                    for t in tiles:
                        e = jnp.exp2(s[j, u, t, :] * rate - shift)
                        p[j, u, t, :] = e.astype(BF16)
                        ds[u, t, :] = (e * (dp[j, u, t, :] - dsum)).astype(BF16)
                    own[k, 1, :, heads[u]] += dot_nn(p[j, u], far[j, c, 1, :, heads[u]])
                    own[k, 0, :, heads[u]] += dot_nn(ds[u], far[j, c, 0, :, heads[u]])
            return carry

        lax.fori_loop(0, levels, one, 0)
        for t in tiles:
            dk_out[b, t, cols(c)] = (own[k, 0, t, :] * scale).astype(BF16)
            dv_out[b, t, cols(c)] = own[k, 1, t, :].astype(BF16)

    def per_chunk(c, carry):
        b = lax.div(c, per)
        k = lax.rem(c, LAG + 1)
        for u in range(GROUP):
            top[u] = jnp.full((1, rows), LOW, F32)
            norm[u] = jnp.zeros((1, rows), F32)
            s[levels, u] = dot_nt(kv[c, 0, :, heads[u]], qd[c, 0, :, heads[u]])
        for u in range(GROUP):
            for t in tiles:
                at = lax.broadcasted_iota(jnp.int32, (TILE, rows), 0) + t.start
                to = lax.broadcasted_iota(jnp.int32, (TILE, rows), 1)
                s[levels, u, t, :] = jnp.where(at <= to, s[levels, u, t, :], LOW)
            absorb(levels, u)

        def score(j, carry):
            held = False
            for ring in range(len(RINGS)):
                held = held | (passes(ring) & (j == RINGS[ring][0]))

            @pl.when((bit(j) == 1) & jnp.logical_not(held))
            def _():
                send_kv(j, c).wait_recv()

            @pl.when(bit(j) == 1)
            def _():
                for u in range(GROUP):
                    s[j, u] = dot_nt(far[j, c, 0, :, heads[u]], qd[c, 0, :, heads[u]])
                for u in range(GROUP):
                    absorb(j, u)
            return carry

        lax.fori_loop(0, levels, score, 0)

        @pl.when(c + 1 < chunks)
        def _():
            pass_on(c + 1)

        for u in range(GROUP):
            norm[u] = top[u] * rate + jnp.log2(norm[u])
            st[c, u:u + 1, :] = norm[u]
            acc[u] = jnp.zeros((HEAD_DIM, rows), F32)
        for u in range(GROUP):
            weigh(levels, u, c, kv.at[c, 1])

        def weighted(j, carry):
            @pl.when(bit(j) == 1)
            def _():
                for u in range(GROUP):
                    weigh(j, u, c, far.at[j, c, 1])
            return carry

        lax.fori_loop(0, levels, weighted, 0)

        for u in range(GROUP):
            mixed = acc[u].astype(BF16).astype(F32)
            lean = qd[c, 1, :, heads[u]].astype(F32).T
            norm[u] = jnp.sum(mixed * lean, axis=0, keepdims=True)
            st[c, GROUP + u:GROUP + u + 1, :] = norm[u]
            at = pl.multiple_of(lax.rem(c, per) * width, width) + u * HEAD_DIM
            attn[b, :, pl.ds(pl.multiple_of(at, HEAD_DIM), HEAD_DIM)] = mixed.T.astype(BF16)
            acc[u] = jnp.zeros((HEAD_DIM, rows), F32)
        for j in range(levels):
            @pl.when(bit(j) == 1)
            def _():
                send_st(j, c).start()

        @pl.when(c + AHEAD < chunks)
        def _():
            issue(c + AHEAD)
            issue_do(c + AHEAD)

        @pl.when(lax.rem(c, per) == per - 1)
        def _():
            for t in range(0, half, width):
                at = pl.ds(pl.multiple_of(far_cols + t, width), width)
                po[b, :, t:t + width] = dot_nn(attn[b], w[:, at]).astype(BF16)
            send_po(b).start()
            for t in range(0, half, width):
                at = pl.ds(pl.multiple_of(own_cols + t, width), width)
                lo[b, :, t:t + width] = dot_nn(attn[b], w[:, at])

        for u in range(GROUP):
            back(levels, u, kv.at[c, 0])
            own[k, 0, :, heads[u]] = dot_nn(ds[u], qd[c, 0, :, heads[u]])
            own[k, 1, :, heads[u]] = dot_nn(p[levels, u], qd[c, 1, :, heads[u]])

        def backward(j, carry):
            @pl.when(bit(j) == 1)
            def _():
                for u in range(GROUP):
                    back(j, u, far.at[j, c, 0])
            return carry

        lax.fori_loop(0, levels, backward, 0)
        for u in range(GROUP):
            at = pl.multiple_of(lax.rem(c, per) * width, width) + u * HEAD_DIM
            at = pl.ds(pl.multiple_of(at, HEAD_DIM), HEAD_DIM)
            dq_out[b, :, at] = (acc[u] * scale).T.astype(BF16)

        @pl.when(c >= LAG)
        def _():
            lower(c - LAG)
        return carry

    pass_on(0)
    lax.fori_loop(0, chunks, per_chunk, 0)
    lax.fori_loop(chunks - LAG, chunks, lambda c, carry: (lower(c), carry)[1], 0)

    for b in range(batch):
        send_po(b).wait_recv()
        for t in tiles:
            lo_out[b, t, :] = (lo[b, t, :] + po_far[b, t, :].astype(F32)).astype(BF16)

    def drain(c, carry):
        for j in range(levels):
            @pl.when(sends_own(j))
            def _():
                send_kv(j, c).wait_send()
        for ring in range(len(RINGS)):
            @pl.when(passes(ring))
            def _():
                pass_kv(ring, c).wait_send()
        for j in range(levels):
            @pl.when(bit(j) == 1)
            def _():
                send_q(j, c).wait_send()
                send_do(j, c).wait_send()
                send_st(j, c).wait_send()
        return carry

    lax.fori_loop(0, chunks, drain, 0)
    for b in range(batch):
        send_og(b).wait_send()
        send_po(b).wait_send()


def put_out(a, b, c, d, a_out, b_out, c_out, d_out, sem):
    copies = []
    for i, (src, dst) in enumerate(((a, a_out), (b, b_out), (c, c_out), (d, d_out))):
        for k in range(src.shape[0]):
            copies.append(pltpu.make_async_copy(src.at[k], dst.at[k], sem.at[i, k]))
            copies[-1].start()
    for copy in copies:
        copy.wait()


def solution(mesh):
    levels = mesh.shape["seq"].bit_length() - 1

    def step(queries, key_states, value_states, output_grad, out_proj):
        batch, rows, half = queries.shape
        width = GROUP * HEAD_DIM
        chunks = batch * (half // width)
        shape = pltpu.VMEM(queries.shape, BF16)
        hbm = pl.BlockSpec(memory_space=pl.ANY)
        dma = pltpu.SemaphoreType.DMA
        results = pl.pallas_call(
            functools.partial(kernel, levels),
            name="butterfly",
            out_shape=[shape] * 4,
            in_specs=[hbm] * 5,
            out_specs=[pl.BlockSpec(memory_space=pltpu.VMEM)] * 4,
            scratch_shapes=[
                pltpu.VMEM((chunks, 2, rows, width), BF16),
                pltpu.VMEM((chunks, 2, rows, width), BF16),
                pltpu.VMEM((levels, chunks, 2, rows, width), BF16),
                pltpu.VMEM(out_proj.shape, BF16),
                pltpu.VMEM((batch, rows, half), BF16),
                pltpu.VMEM((batch, rows, half), BF16),
                pltpu.VMEM((batch, rows, half), BF16),
                pltpu.VMEM((levels + 1, GROUP, rows, rows), F32),
                pltpu.VMEM((levels + 1, GROUP, rows, rows), BF16),
                pltpu.VMEM((levels + 1, GROUP, rows, rows), F32),
                pltpu.VMEM((GROUP, rows, rows), BF16),
                pltpu.VMEM((GROUP, 1, rows), F32),
                pltpu.VMEM((GROUP, 1, rows), F32),
                pltpu.VMEM((GROUP, HEAD_DIM, rows), F32),
                pltpu.VMEM((LAG + 1, 2, rows, width), F32),
                pltpu.VMEM((batch, rows, half), BF16),
                pltpu.VMEM((batch, rows, half), BF16),
                pltpu.VMEM((batch, rows, half), F32),
                pltpu.VMEM((chunks, 8, rows), F32),
                pltpu.VMEM((levels, chunks, 8, rows), F32),
                dma((chunks,)),
                dma((chunks, 2)),
                dma((batch,)),
                dma,
                dma((batch,)),
                dma((batch,)),
                dma((batch,)),
                dma((batch,)),
                dma((levels, chunks)),
                dma((levels, chunks)),
                dma((levels, chunks)),
                dma((levels, chunks)),
                dma((levels, chunks)),
                dma((levels, chunks)),
                dma((len(RINGS), chunks)),
            ],
            compiler_params=pltpu.CompilerParams(
                collective_id=0, has_side_effects=True, vmem_limit_bytes=119 << 19
            ),
        )(queries, key_states, value_states, output_grad, out_proj)
        return tuple(pl.pallas_call(
            put_out,
            name="put_out",
            out_shape=[jax.ShapeDtypeStruct(queries.shape, BF16)] * 4,
            in_specs=[pl.BlockSpec(memory_space=pltpu.VMEM)] * 4,
            out_specs=[hbm] * 4,
            scratch_shapes=[dma((4, batch))],
            compiler_params=pltpu.CompilerParams(vmem_limit_bytes=1 << 20),
        )(*results))

    act = P(None, "seq", "head")
    return jax.shard_map(
        step, mesh=mesh, in_specs=(act, act, act, act, P("head", None)),
        out_specs=(act,) * 4, check_vma=False,
    )
```

```python
import functools
import math

import jax
import jax.numpy as jnp
from jax import lax
from jax.experimental import pallas as pl
from jax.experimental.pallas import tpu as pltpu
from jax.sharding import PartitionSpec as P

HEAD_DIM = 128
GROUP = 2
MESH = pl.DeviceIdType.MESH
F32 = jnp.float32
BF16 = jnp.bfloat16
LOW = -1e30
TILE = 32
RINGS = ((2, 3), (4, 5))
AHEAD = 2
AHEAD_KV = 8
OG_AT = 1
LAG = 3


def dot_nt(a, b):
    return lax.dot_general(a, b, (((1,), (1,)), ((), ())), preferred_element_type=F32)


def dot_nn(a, b):
    return lax.dot_general(a, b, (((1,), (0,)), ((), ())), preferred_element_type=F32)


def dot_tn(a, b):
    return lax.dot_general(a, b, (((0,), (0,)), ((), ())), preferred_element_type=F32)


def kernel(
    levels, q_in, k_in, v_in, og_in, w_in, lo_out, dq_out, dk_out, dv_out,
    kv, qd, far, w, og, og_far, attn, s, p, dp, ds, top, norm, acc, own, po, po_far, lo, st, st_far,
    ld_q, ld_kv, ld_og, ld_w, og_send, og_recv, po_send, po_recv,
    kv_send, kv_recv, do_send, do_recv, st_send, st_recv, pass_send,
):
    me = lax.axis_index("seq")
    hd = lax.axis_index("head")
    chunks, _, rows, width = kv.shape
    batch = og.shape[0]
    half = og.shape[2]
    per = chunks // batch
    scale = HEAD_DIM ** -0.5
    rate = scale * math.log2(math.e)
    own_cols = pl.multiple_of(hd * half, half)
    far_cols = pl.multiple_of((1 - hd) * half, half)

    def bit(j):
        return lax.rem(lax.shift_right_logical(me, j), 2)

    def partner(j):
        return me + (1 - 2 * bit(j)) * (1 << j)

    def cols(c):
        return pl.ds(pl.multiple_of(lax.rem(c, per) * width, width), width)

    def load_kv(c, i):
        src = (k_in, v_in)[i].at[lax.div(c, per), :, cols(c)]
        return pltpu.make_async_copy(src, kv.at[c, i], ld_kv.at[c, i])

    def load_q(c):
        return pltpu.make_async_copy(q_in.at[lax.div(c, per), :, cols(c)], qd.at[c, 0], ld_q.at[c])

    def load_og(b):
        return pltpu.make_async_copy(og_in.at[b], og.at[b], ld_og.at[b])

    load_w = pltpu.make_async_copy(w_in, w, ld_w)

    def to_head(src, dst, send, recv):
        return pltpu.make_async_remote_copy(
            src, dst, send, recv, device_id=(me, 1 - hd), device_id_type=MESH)

    def to_partner(j, src, dst, send, recv):
        return pltpu.make_async_remote_copy(
            src, dst, send, recv, device_id=(partner(j), hd), device_id_type=MESH)

    def send_og(b):
        return to_head(og_in.at[b], og_far.at[b], og_send.at[b], og_recv.at[b])

    def send_po(b, n):
        return to_head(po.at[b, n], po_far.at[b, n], po_send.at[b, n], po_recv.at[b, n])

    def send_kv(j, c):
        return to_partner(j, kv.at[c], far.at[j, c], kv_send.at[j, c], kv_recv.at[j, c])

    def passes(ring):
        near, apart = RINGS[ring]
        return (bit(near) == 1) & (bit(apart) == 0)

    def opposite(ring):
        near, apart = RINGS[ring]
        return partner(near) + partner(apart) - me

    def pass_kv(ring, c):
        near, apart = RINGS[ring]
        return pltpu.make_async_remote_copy(
            far.at[near, c], far.at[apart, c], pass_send.at[ring, c], kv_recv.at[apart, c],
            device_id=(opposite(ring), hd), device_id_type=MESH)

    def pass_on(c):
        for ring in range(len(RINGS)):
            @pl.when(passes(ring))
            def _():
                send_kv(RINGS[ring][0], c).wait_recv()
                pass_kv(ring, c).start()

    def sends_own(j):
        sender = bit(j) == 0
        for near, apart in RINGS:
            if j == apart:
                sender = sender & (bit(near) == 1)
        return sender

    def send_q(j, c):
        return to_partner(j, qd.at[c, 0], far.at[j, c, 0], kv_send.at[j, c], kv_recv.at[j, c])

    def send_do(j, c):
        return to_partner(j, qd.at[c, 1], far.at[j, c, 1], do_send.at[j, c], do_recv.at[j, c])

    def send_st(j, c):
        return to_partner(j, st.at[c], st_far.at[j, c], st_send.at[j, c], st_recv.at[j, c])

    def start_loads(c, carry):
        load_kv(c, 0).start()
        load_kv(c, 1).start()
        load_q(c).start()
        return carry

    lax.fori_loop(0, chunks, start_loads, 0)
    for b in range(batch):
        load_og(b).start()
    load_w.start()

    barrier = pltpu.get_barrier_semaphore()
    for j in range(levels):
        pl.semaphore_signal(barrier, inc=1, device_id=(partner(j), hd), device_id_type=MESH)
    for ring in range(len(RINGS)):
        pl.semaphore_signal(barrier, inc=1, device_id=(opposite(ring), hd), device_id_type=MESH)
    pl.semaphore_signal(barrier, inc=1, device_id=(me, 1 - hd), device_id_type=MESH)
    st[...] = jnp.zeros_like(st)
    pl.semaphore_wait(barrier, levels + 1 + len(RINGS))

    heads = [slice(u * HEAD_DIM, (u + 1) * HEAD_DIM) for u in range(GROUP)]
    tiles = [slice(t, t + TILE) for t in range(0, rows, TILE)]

    def issue_kv(c):
        load_kv(c, 0).wait()
        load_kv(c, 1).wait()
        for j in range(levels):
            @pl.when(sends_own(j))
            def _():
                send_kv(j, c).start()

    def issue(c):
        load_q(c).wait()
        for j in range(levels):
            @pl.when(bit(j) == 1)
            def _():
                send_q(j, c).start()

    def issue_do(c):
        b = lax.div(c, per)

        @pl.when(lax.rem(c, per) == 0)
        def _():
            send_og(b).wait_recv()

        w_rows = pl.ds(pl.multiple_of(lax.rem(c, per) * width, width), width)
        qd[c, 1] = (
            dot_nt(og[b], w[w_rows, pl.ds(own_cols, half)])
            + dot_nt(og_far[b], w[w_rows, pl.ds(far_cols, half)])
        ).astype(BF16)
        for j in range(levels):
            @pl.when(bit(j) == 1)
            def _():
                send_do(j, c).start()

    send_og(0).start()

    def start_sends(c, carry):
        issue_kv(c)

        @pl.when(c < AHEAD)
        def _():
            issue(c)
        if batch > 1:
            @pl.when(c == OG_AT)
            def _():
                for b in range(1, batch):
                    send_og(b).start()
        return carry

    lax.fori_loop(0, AHEAD_KV, start_sends, 0)
    for b in range(batch):
        load_og(b).wait()
    load_w.wait()
    lax.fori_loop(0, AHEAD, lambda c, carry: (issue_do(c), carry)[1], 0)

    def absorb(slot, u):
        peak = s[slot, u, tiles[0], :]
        for t in tiles[1:]:
            peak = jnp.maximum(peak, s[slot, u, t, :])
        old = top[u]
        new = jnp.maximum(old, jnp.max(peak, axis=0, keepdims=True))
        total = None
        for t in tiles:
            e = jnp.exp2((s[slot, u, t, :] - new) * rate)
            total = e if total is None else total + e
        norm[u] = norm[u] * jnp.exp2((old - new) * rate) + jnp.sum(total, axis=0, keepdims=True)
        top[u] = new

    def weigh(slot, u, c, value_ref):
        shift = norm[u]
        dp[slot, u] = dot_nt(value_ref[:, heads[u]], qd[c, 1, :, heads[u]])
        for t in tiles:
            e = jnp.exp2(s[slot, u, t, :] * rate - shift)
            s[slot, u, t, :] = e
            p[slot, u, t, :] = e.astype(BF16)
        acc[u] += dot_tn(value_ref[:, heads[u]], p[slot, u])

    def back(slot, u, key_ref):
        dsum = norm[u]
        for t in tiles:
            ds[u, t, :] = (s[slot, u, t, :] * (dp[slot, u, t, :] - dsum)).astype(BF16)
        acc[u] += dot_tn(key_ref[:, heads[u]], ds[u])

    def lower(c):
        b = lax.div(c, per)
        k = lax.rem(c, LAG + 1)

        def one(j, carry):
            @pl.when(bit(j) == 0)
            def _():
                send_q(j, c).wait_recv()
                send_do(j, c).wait_recv()
                send_st(j, c).wait_recv()
                for u in range(GROUP):
                    s[j, u] = dot_nt(kv[c, 0, :, heads[u]], far[j, c, 0, :, heads[u]])
                    dp[j, u] = dot_nt(kv[c, 1, :, heads[u]], far[j, c, 1, :, heads[u]])
                for u in range(GROUP):
                    shift = st_far[j, c, u:u + 1, :]
                    dsum = st_far[j, c, GROUP + u:GROUP + u + 1, :]
                    for t in tiles:
                        e = jnp.exp2(s[j, u, t, :] * rate - shift)
                        p[j, u, t, :] = e.astype(BF16)
                        ds[u, t, :] = (e * (dp[j, u, t, :] - dsum)).astype(BF16)
                    own[k, 1, :, heads[u]] += dot_nn(p[j, u], far[j, c, 1, :, heads[u]])
                    own[k, 0, :, heads[u]] += dot_nn(ds[u], far[j, c, 0, :, heads[u]])
            return carry

        lax.fori_loop(0, levels, one, 0)
        for t in tiles:
            dk_out[b, t, cols(c)] = (own[k, 0, t, :] * scale).astype(BF16)
            dv_out[b, t, cols(c)] = own[k, 1, t, :].astype(BF16)

    def per_chunk(c, carry):
        b = lax.div(c, per)
        k = lax.rem(c, LAG + 1)
        for u in range(GROUP):
            top[u] = jnp.full((1, rows), LOW, F32)
            norm[u] = jnp.zeros((1, rows), F32)
            s[levels, u] = dot_nt(kv[c, 0, :, heads[u]], qd[c, 0, :, heads[u]])
        for u in range(GROUP):
            for t in tiles:
                at = lax.broadcasted_iota(jnp.int32, (TILE, rows), 0) + t.start
                to = lax.broadcasted_iota(jnp.int32, (TILE, rows), 1)
                s[levels, u, t, :] = jnp.where(at <= to, s[levels, u, t, :], LOW)
            absorb(levels, u)

        def score(j, carry):
            held = False
            for ring in range(len(RINGS)):
                held = held | (passes(ring) & (j == RINGS[ring][0]))

            @pl.when((bit(j) == 1) & jnp.logical_not(held))
            def _():
                send_kv(j, c).wait_recv()

            @pl.when(bit(j) == 1)
            def _():
                for u in range(GROUP):
                    s[j, u] = dot_nt(far[j, c, 0, :, heads[u]], qd[c, 0, :, heads[u]])
                for u in range(GROUP):
                    absorb(j, u)
            return carry

        lax.fori_loop(0, levels, score, 0)

        @pl.when(c + 1 < chunks)
        def _():
            pass_on(c + 1)

        for u in range(GROUP):
            norm[u] = top[u] * rate + jnp.log2(norm[u])
            st[c, u:u + 1, :] = norm[u]
            acc[u] = jnp.zeros((HEAD_DIM, rows), F32)
        for u in range(GROUP):
            weigh(levels, u, c, kv.at[c, 1])

        def weighted(j, carry):
            @pl.when(bit(j) == 1)
            def _():
                for u in range(GROUP):
                    weigh(j, u, c, far.at[j, c, 1])
            return carry

        lax.fori_loop(0, levels, weighted, 0)

        for u in range(GROUP):
            mixed = acc[u].astype(BF16).astype(F32)
            lean = qd[c, 1, :, heads[u]].astype(F32).T
            norm[u] = jnp.sum(mixed * lean, axis=0, keepdims=True)
            st[c, GROUP + u:GROUP + u + 1, :] = norm[u]
            at = pl.multiple_of(lax.rem(c, per) * width, width) + u * HEAD_DIM
            attn[b, :, pl.ds(pl.multiple_of(at, HEAD_DIM), HEAD_DIM)] = mixed.T.astype(BF16)
            acc[u] = jnp.zeros((HEAD_DIM, rows), F32)
        for j in range(levels):
            @pl.when(bit(j) == 1)
            def _():
                send_st(j, c).start()

        @pl.when(c + AHEAD < chunks)
        def _():
            issue(c + AHEAD)
            issue_do(c + AHEAD)

        @pl.when(lax.rem(c, per) == per - 1)
        def _():
            for t in range(0, half, width):
                at = pl.ds(pl.multiple_of(far_cols + t, width), width)
                po[b, t // width] = dot_nn(attn[b], w[:, at]).astype(BF16)
                send_po(b, t // width).start()
            for t in range(0, half, width):
                at = pl.ds(pl.multiple_of(own_cols + t, width), width)
                lo[b, :, t:t + width] = dot_nn(attn[b], w[:, at])

        for u in range(GROUP):
            back(levels, u, kv.at[c, 0])
            own[k, 0, :, heads[u]] = dot_nn(ds[u], qd[c, 0, :, heads[u]])
            own[k, 1, :, heads[u]] = dot_nn(p[levels, u], qd[c, 1, :, heads[u]])

        def backward(j, carry):
            @pl.when(bit(j) == 1)
            def _():
                for u in range(GROUP):
                    back(j, u, far.at[j, c, 0])
            return carry

        lax.fori_loop(0, levels, backward, 0)
        for u in range(GROUP):
            at = pl.multiple_of(lax.rem(c, per) * width, width) + u * HEAD_DIM
            at = pl.ds(pl.multiple_of(at, HEAD_DIM), HEAD_DIM)
            dq_out[b, :, at] = (acc[u] * scale).T.astype(BF16)

        @pl.when(c >= LAG)
        def _():
            lower(c - LAG)
        return carry

    pass_on(0)
    lax.fori_loop(0, chunks, per_chunk, 0)
    lax.fori_loop(chunks - LAG, chunks - 1, lambda c, carry: (lower(c), carry)[1], 0)
    for b in range(batch):
        for n in range(half // width):
            send_po(b, n).wait_recv()
            at = slice(n * width, (n + 1) * width)
            for t in tiles:
                lo_out[b, t, at] = (lo[b, t, at] + po_far[b, n, t, :].astype(F32)).astype(BF16)

    lower(chunks - 1)

    def drain(c, carry):
        for j in range(levels):
            @pl.when(sends_own(j))
            def _():
                send_kv(j, c).wait_send()
        for ring in range(len(RINGS)):
            @pl.when(passes(ring))
            def _():
                pass_kv(ring, c).wait_send()
        for j in range(levels):
            @pl.when(bit(j) == 1)
            def _():
                send_q(j, c).wait_send()
                send_do(j, c).wait_send()
                send_st(j, c).wait_send()
        return carry

    lax.fori_loop(0, chunks, drain, 0)
    for b in range(batch):
        send_og(b).wait_send()
        for n in range(half // width):
            send_po(b, n).wait_send()


def put_out(a, b, c, d, a_out, b_out, c_out, d_out, sem):
    copies = []
    for i, (src, dst) in enumerate(((a, a_out), (b, b_out), (c, c_out), (d, d_out))):
        for k in range(src.shape[0]):
            copies.append(pltpu.make_async_copy(src.at[k], dst.at[k], sem.at[i, k]))
            copies[-1].start()
    for copy in copies:
        copy.wait()


def solution(mesh):
    levels = mesh.shape["seq"].bit_length() - 1

    def step(queries, key_states, value_states, output_grad, out_proj):
        batch, rows, half = queries.shape
        width = GROUP * HEAD_DIM
        chunks = batch * (half // width)
        shape = pltpu.VMEM(queries.shape, BF16)
        hbm = pl.BlockSpec(memory_space=pl.ANY)
        dma = pltpu.SemaphoreType.DMA
        results = pl.pallas_call(
            functools.partial(kernel, levels),
            name="butterfly",
            out_shape=[shape] * 4,
            in_specs=[hbm] * 5,
            out_specs=[pl.BlockSpec(memory_space=pltpu.VMEM)] * 4,
            scratch_shapes=[
                pltpu.VMEM((chunks, 2, rows, width), BF16),
                pltpu.VMEM((chunks, 2, rows, width), BF16),
                pltpu.VMEM((levels, chunks, 2, rows, width), BF16),
                pltpu.VMEM(out_proj.shape, BF16),
                pltpu.VMEM((batch, rows, half), BF16),
                pltpu.VMEM((batch, rows, half), BF16),
                pltpu.VMEM((batch, rows, half), BF16),
                pltpu.VMEM((levels + 1, GROUP, rows, rows), F32),
                pltpu.VMEM((levels + 1, GROUP, rows, rows), BF16),
                pltpu.VMEM((levels + 1, GROUP, rows, rows), F32),
                pltpu.VMEM((GROUP, rows, rows), BF16),
                pltpu.VMEM((GROUP, 1, rows), F32),
                pltpu.VMEM((GROUP, 1, rows), F32),
                pltpu.VMEM((GROUP, HEAD_DIM, rows), F32),
                pltpu.VMEM((LAG + 1, 2, rows, width), F32),
                pltpu.VMEM((batch, half // width, rows, width), BF16),
                pltpu.VMEM((batch, half // width, rows, width), BF16),
                pltpu.VMEM((batch, rows, half), F32),
                pltpu.VMEM((chunks, 8, rows), F32),
                pltpu.VMEM((levels, chunks, 8, rows), F32),
                dma((chunks,)),
                dma((chunks, 2)),
                dma((batch,)),
                dma,
                dma((batch,)),
                dma((batch,)),
                dma((batch, half // width)),
                dma((batch, half // width)),
                dma((levels, chunks)),
                dma((levels, chunks)),
                dma((levels, chunks)),
                dma((levels, chunks)),
                dma((levels, chunks)),
                dma((levels, chunks)),
                dma((len(RINGS), chunks)),
            ],
            compiler_params=pltpu.CompilerParams(
                collective_id=0, has_side_effects=True, vmem_limit_bytes=119 << 19
            ),
        )(queries, key_states, value_states, output_grad, out_proj)
        return tuple(pl.pallas_call(
            put_out,
            name="put_out",
            out_shape=[jax.ShapeDtypeStruct(queries.shape, BF16)] * 4,
            in_specs=[pl.BlockSpec(memory_space=pltpu.VMEM)] * 4,
            out_specs=[hbm] * 4,
            scratch_shapes=[dma((4, batch))],
            compiler_params=pltpu.CompilerParams(vmem_limit_bytes=1 << 20),
        )(*results))

    act = P(None, "seq", "head")
    return jax.shard_map(
        step, mesh=mesh, in_specs=(act, act, act, act, P("head", None)),
        out_specs=(act,) * 4, check_vma=False,
    )
```
